32 devices in a mesh: cohort: 2 (over x), grp: 4 (over z), vox: 4 (over y, core).
Axes of the slice: x: 2, y: 2, z: 4, core: 2. Of those that a mesh axis runs over, the one named last changes fastest.
Arguments:
- probes: bfloat16 [16384, 256], P(('cohort', 'grp', 'vox')), parts along dimension 0, may hold values from -6 to 6
- blocks: bfloat16 [512, 4, 128, 128], P(('cohort', 'grp', 'vox')), parts along dimension 0, may hold values from -0.25 to 0.25
- pattern: int32 [512, 4], P(('cohort', 'grp', 'vox')), parts along dimension 0, may hold values from 0 to 31, as said below
- scale_exp: int32 [512, 4], P(('cohort', 'grp', 'vox')), parts along dimension 0, may hold values from -2 to 2
- noise: float32 [512, 128], P(('cohort', 'grp', 'vox')), parts along dimension 0, may hold values from 0.1 to 1
Outputs:
- hessian_probes: float32 [16384, 256], P(('cohort', 'grp', 'vox')), parts along dimension 0
The draws below stay inside these ranges and needn't reach their ends.
There are 2 independent parts, one for each index of `cohort`. The reference program is written for one: setup_inputs(seed, part) draws one part's arguments, and reference() takes and returns one part's arrays. A program takes and returns all parts, laid end to end along the dimension named above; each array names one. Nothing has to cross between parts.
Inputs may be any that keep to these rules, and one draw needn't show every extreme that they name: pattern is below 16 in the last group's rows; other rows may reach into the next group's parameter blocks.
All inputs are finite; a program needn't handle non-finite values.
Results may differ from the reference program's by a relative error of at most 0.0016.
Values may be sent and summed in bfloat16 or wider, within the bound.
No kernel may reach another device: no remote copies, remote signals or barrier semaphores. Data moves between devices by JAX's collectives and lax.ppermute only.
A program may use at most 128 MiB of HBM per device.

```python
import math
import jax
import jax.numpy as jnp
from jax import lax

BLK = 128
PROBES = 256
NNZ = 4
ROWS_DEV = 16
GROUP_BLOCKS = 16
PARAM_BLOCKS = 64
PARAMS = 8192
BLOCK_ROWS = 256
N_GRP = 4
N_VOX = 4


def draw_pattern(key, part):
    rows = jnp.arange(BLOCK_ROWS)
    group_id = rows // (ROWS_DEV * N_VOX)
    reach = jnp.where(group_id == N_GRP - 1, GROUP_BLOCKS, 2 * GROUP_BLOCKS)
    raw = jax.random.randint(key, (BLOCK_ROWS, NNZ), 0, 1 << 20)
    columns = raw % reach[:, None]
    columns = columns.at[0, 0].set(2 * GROUP_BLOCKS - 1).at[0, 1].set(0)
    return columns.astype(jnp.int32)


def place_ends(result, stream_key, smallest, top_value):
    dims = result.shape
    place = [jax.random.randint(jax.random.fold_in(stream_key, axis), (), 0, dims[axis]) for axis in range(len(dims))]
    result = result.at[tuple(place)].set(smallest)
    longest = dims.index(max(dims))
    place[longest] = (place[longest] + 1) % dims[longest]
    return result.at[tuple(place)].set(top_value)


def block_scale(stream_key, shape, split, least, top_value):
    def one(position, shards_of):
        heights = jax.random.uniform(jax.random.fold_in(jax.random.fold_in(stream_key, 6), position), (shards_of,), jnp.float32, least / len(split), top_value / len(split))
        return jnp.repeat(jnp.exp(heights), shape[position] // shards_of).reshape((-1,) + (1,) * (len(shape) - position - 1))

    gain = one(*split[0])
    for cut in split[1:]:
        gain = gain * one(*cut)
    return gain


def gaussian(own_key, shape, deviation, most, cuts=(), dtype=jnp.bfloat16):
    entries = deviation * jax.random.normal(own_key, shape, jnp.float32)
    if cuts:
        entries = entries * block_scale(own_key, shape, cuts, -0.22, 0.18)
    return jnp.clip(entries, -most, most).astype(dtype)


def setup_inputs(seed: int = 0, part: int = 0) -> dict:
    seeds = jax.random.split(jax.random.key(seed), 6)
    part_splits = jax.random.split(jax.random.fold_in(seeds[5], part), 6)
    probes = gaussian(part_splits[0], (PARAMS, PROBES), 1.0, 6.0, ((0, 16),))
    blocks = gaussian(part_splits[1], (BLOCK_ROWS, NNZ, BLK, BLK), (BLK * NNZ) ** -0.5, 0.25, ((0, 16),))
    pattern = draw_pattern(jax.random.fold_in(jax.random.fold_in(seeds[5], part), 71), part)
    scale_exp = place_ends(jax.random.randint(part_splits[3], (BLOCK_ROWS, NNZ), -2, 3), jax.random.fold_in(part_splits[3], 1), -2, 2).astype(jnp.int32)
    noise = jnp.clip(jnp.exp(math.log(1.0) - 2.3025851 * jax.random.uniform(part_splits[4], (BLOCK_ROWS, BLK), jnp.float32) ** block_scale(part_splits[4], (BLOCK_ROWS, BLK), ((0, 16),), -0.2, 0.2)), 0.1, 1.0)
    return dict(probes=probes, blocks=blocks, pattern=pattern, scale_exp=scale_exp, noise=noise)


def reference(probes, blocks, pattern, scale_exp, noise):
    panels = probes.reshape(PARAM_BLOCKS, BLK, PROBES)
    devices_all = N_GRP * N_VOX
    group_of = (jnp.arange(devices_all) // N_VOX).astype(jnp.int32)
    items = (blocks.reshape(devices_all, ROWS_DEV, NNZ, BLK, BLK),
             pattern.reshape(devices_all, ROWS_DEV, NNZ),
             scale_exp.reshape(devices_all, ROWS_DEV, NNZ),
             noise.reshape(devices_all, ROWS_DEV, BLK),
             group_of)

    def step(total, item):
        block_vals, local_cols, expo, weights, group_id = item
        columns = (local_cols + group_id * GROUP_BLOCKS).astype(jnp.int32)
        scales = jnp.exp2(expo.astype(jnp.float32))
        forward = jnp.zeros((ROWS_DEV, BLK, PROBES), jnp.float32)
        for slot in range(NNZ):
            picked = panels[columns[:, slot]].astype(jnp.float32)
            product = jnp.einsum("rab,rbk->rak", block_vals[:, slot].astype(jnp.float32), picked)
            forward = forward + product * scales[:, slot, None, None]
        weighted = (weights[:, :, None] * forward).astype(jnp.bfloat16)
        weighted = lax.optimization_barrier(weighted).astype(jnp.float32)
        for slot in range(NNZ):
            back = jnp.einsum("rab,rak->rbk", block_vals[:, slot].astype(jnp.float32), weighted)
            total = total.at[columns[:, slot]].add(back * scales[:, slot, None, None])
        return total, None

    start = jnp.zeros((PARAM_BLOCKS, BLK, PROBES), jnp.float32)
    total = lax.scan(step, start, items)[0]
    return total.reshape(PARAMS, PROBES)
```

```python
import functools

import jax
import jax.numpy as jnp
from jax import lax
from jax.experimental import pallas as pl
from jax.experimental.pallas import tpu as pltpu
from jax.sharding import PartitionSpec as P

AXES = ("cohort", "grp", "vox")
CODE_BITS = 14


def core_swap(array):
    devices = lax.axis_size("vox")
    return lax.ppermute(array, "vox", [(i, i ^ 1) for i in range(devices)])


def hop(array, group_by, chip_by):
    groups, devices = lax.axis_size("grp"), lax.axis_size("vox")
    chips = devices // 2
    pairs = []
    for g in range(groups):
        for y in range(chips):
            for c in range(2):
                to = g + group_by
                if 0 <= to < groups:
                    target = 2 * ((y + chip_by) % chips) + c
                    pairs.append((g * devices + 2 * y + c, to * devices + target))
    return lax.ppermute(array, ("grp", "vox"), pairs)


def prepare_kernel(scale_ref, blocks_ref, wide_ref, tall_ref):
    rows, count, width, _ = blocks_ref.shape
    first = pl.program_id(0) * rows
    for r in range(rows):
        for n in range(count):
            scale = scale_ref[(first + r) * count + n]
            block = (blocks_ref[r, n].astype(jnp.float32) * scale).astype(jnp.bfloat16)
            wide_ref[r, :, n * width:(n + 1) * width] = block
            tall_ref[r, n * width:(n + 1) * width, :] = block.T


def prepare(scales, blocks):
    rows, count, width, _ = blocks.shape
    step = 4
    return pl.pallas_call(
        prepare_kernel,
        grid_spec=pltpu.PrefetchScalarGridSpec(
            num_scalar_prefetch=1,
            grid=(rows // step,),
            in_specs=[pl.BlockSpec((step, count, width, width), lambda i, s: (i, 0, 0, 0))],
            out_specs=[
                pl.BlockSpec((step, width, count * width), lambda i, s: (i, 0, 0)),
                pl.BlockSpec((step, count * width, width), lambda i, s: (i, 0, 0)),
            ],
        ),
        out_shape=[
            jax.ShapeDtypeStruct((rows, width, count * width), jnp.bfloat16),
            jax.ShapeDtypeStruct((rows, count * width, width), jnp.bfloat16),
        ],
        name="prepare",
        cost_estimate=pl.CostEstimate(flops=0, transcendentals=0, bytes_accessed=3 * blocks.size * 2),
    )(scales, blocks)


def apply_kernel(shards, pick_ref, put_ref, wide_ref, tall_ref, noise_ref, *refs):
    shard_refs = refs[:shards]
    sib_ref, keep_ref, panels, total, in_sem, out_sem = refs[shards:]
    rows, width, deep = wide_ref.shape
    count = deep // width
    per = shard_refs[0].shape[0] // width
    cols = noise_ref.shape[2]
    copies = [
        pltpu.make_async_copy(ref, panels.at[pl.ds(i * per * width, per * width)], in_sem.at[i])
        for i, ref in enumerate(shard_refs)
    ]
    for copy in copies:
        copy.start()
    total[...] = jnp.zeros_like(total)
    for copy in copies:
        copy.wait()

    def row(r, carry):
        picked = jnp.concatenate(
            [
                panels[pl.ds(pl.multiple_of(pick_ref[r * count + n] * width, width), width), :]
                for n in range(count)
            ],
            axis=0,
        )
        forward = jnp.dot(wide_ref[r], picked, preferred_element_type=jnp.float32)
        weight = noise_ref[r]
        parts = [weight * forward[:, k:k + cols] for k in range(0, forward.shape[1], cols)]
        weighted = jnp.concatenate(parts, axis=1).astype(jnp.bfloat16)
        back = jnp.dot(tall_ref[r], weighted, preferred_element_type=jnp.float32)
        for n in range(count):
            spot = pl.ds(pl.multiple_of(put_ref[r * count + n] * width, width), width)
            total[spot, :] += back[n * width:(n + 1) * width, :]
        return carry

    lax.fori_loop(0, rows, row, 0)
    half = total.shape[0] // 2
    outs = [
        pltpu.make_async_copy(total.at[pl.ds(0, half)], sib_ref, out_sem.at[0]),
        pltpu.make_async_copy(total.at[pl.ds(half, half)], keep_ref, out_sem.at[1]),
    ]
    for copy in outs:
        copy.start()
    for copy in outs:
        copy.wait()


def apply(pick, put, wide, tall, noise, shards):
    rows, width, deep = wide.shape
    cols = shards[0].shape[1]
    held = sum(s.shape[0] for s in shards)
    whole = pl.BlockSpec(memory_space=pltpu.VMEM)
    part = jax.ShapeDtypeStruct((held // 2, cols), jnp.float32)
    return pl.pallas_call(
        functools.partial(apply_kernel, len(shards)),
        grid_spec=pltpu.PrefetchScalarGridSpec(
            num_scalar_prefetch=2,
            grid=(),
            in_specs=[whole, whole, whole] + [pl.BlockSpec(memory_space=pl.ANY)] * len(shards),
            out_specs=[pl.BlockSpec(memory_space=pl.ANY)] * 2,
            scratch_shapes=[
                pltpu.VMEM((held, cols), jnp.bfloat16),
                pltpu.VMEM((held, cols), jnp.float32),
                pltpu.SemaphoreType.DMA((len(shards),)),
                pltpu.SemaphoreType.DMA((2,)),
            ],
        ),
        out_shape=[part, part],
        name="apply",
        cost_estimate=pl.CostEstimate(
            flops=4 * rows * width * deep * cols, transcendentals=0, bytes_accessed=4 * held * cols
        ),
    )(pick, put, wide, tall, noise, *shards)


def code_kernel(keep_ref, got_ref, own_ref, *code_refs):
    size = own_ref.shape[0]
    own_ref[...] = keep_ref[:size, :] + got_ref[:size, :]
    for i, code_ref in enumerate(code_refs):
        rows = slice((i + 1) * size, (i + 2) * size)
        value = keep_ref[rows, :] + got_ref[rows, :]
        most = jnp.max(jnp.abs(value), axis=0, keepdims=True)
        power = jnp.floor(jnp.log2(jnp.maximum(most, 1e-30))) + 1.0
        steps = jnp.round(value * jnp.exp2(CODE_BITS - power))
        code_ref[:size, :] = steps.astype(jnp.int32).astype(jnp.int16)
        mark = jnp.broadcast_to(power, (code_ref.shape[0] - size, power.shape[1]))
        code_ref[size:, :] = mark.astype(jnp.int32).astype(jnp.int16)


def code(keep, got, messages):
    size, cols = keep.shape[0] // (messages + 1), keep.shape[1]
    whole = pl.BlockSpec(memory_space=pltpu.VMEM)
    return pl.pallas_call(
        code_kernel,
        in_specs=[whole, whole],
        out_specs=[whole] * (messages + 1),
        out_shape=[jax.ShapeDtypeStruct((size, cols), jnp.float32)]
        + [jax.ShapeDtypeStruct((size + 16, cols), jnp.int16)] * messages,
        name="code",
        cost_estimate=pl.CostEstimate(flops=0, transcendentals=0, bytes_accessed=keep.size * 12),
    )(keep, got)


def join_kernel(own_ref, *refs):
    out_ref = refs[-1]
    size = own_ref.shape[0]
    value = own_ref[...]
    for code_ref in refs[:-1]:
        power = code_ref[size:, :].astype(jnp.int32).astype(jnp.float32)[:1, :]
        steps = code_ref[:size, :].astype(jnp.int32).astype(jnp.float32)
        value = value + steps * jnp.exp2(power - CODE_BITS)
    out_ref[...] = value


def join(own, codes):
    whole = pl.BlockSpec(memory_space=pltpu.VMEM)
    return pl.pallas_call(
        join_kernel,
        in_specs=[whole] * (1 + len(codes)),
        out_specs=whole,
        out_shape=jax.ShapeDtypeStruct(own.shape, jnp.float32),
        name="join",
        cost_estimate=pl.CostEstimate(flops=0, transcendentals=0, bytes_accessed=own.size * 14),
    )(own, *codes)


def local(probes, blocks, pattern, scale_exp, noise):
    rows_here, count, width, _ = blocks.shape
    chips = lax.axis_size("vox") // 2
    per = probes.shape[0] // width
    group = per * 2 * chips
    me = lax.axis_index("vox")
    chip, core = me // 2, me % 2

    far = [hop(probes, -1, -d) for d in range(1, chips)]
    near = [hop(probes, 0, -d) for d in range(1, chips)]
    ahead = hop(probes, -1, 0)
    mine = [probes] + near + [ahead] + far
    shards = []
    for shard in mine:
        shards += [shard, core_swap(shard)]

    column = pattern.reshape(-1)
    is_next = (column >= group).astype(jnp.int32)
    inside = column - is_next * group
    owner = inside // per
    distance = (owner // 2 - chip) % chips
    other = (owner % 2) ^ core
    within = inside % per
    pick = ((is_next * chips + distance) * 2 + other) * per + within
    put = ((1 - other) * 2 * chips + is_next * chips + distance) * per + within
    scales = jnp.exp2(scale_exp.reshape(-1).astype(jnp.float32))
    wide, tall = prepare(scales, blocks)
    weight = jnp.broadcast_to(noise[:, :, None], (rows_here, width, 128))

    sib, keep = apply(pick, put, wide, tall, weight, shards)
    got = core_swap(sib)
    own, *codes = code(keep, got, 2 * chips - 1)
    sent = []
    for i, value in enumerate(codes, start=1):
        sent.append(hop(value, i // chips, i % chips))
    return join(own, sent)


def solution(mesh):
    in_specs = (
        P(AXES, None),
        P(AXES, None, None, None),
        P(AXES, None),
        P(AXES, None),
        P(AXES, None),
    )
    out_specs = P(AXES, None)
    return jax.shard_map(local, mesh=mesh, in_specs=in_specs, out_specs=out_specs, check_vma=False)
```
